512 devices in a mesh: dom: 64 (over z, x), sub: 8 (over y, core).
Axes of the slice: x: 4, y: 4, z: 16, core: 2. Of those that a mesh axis runs over, the one named last changes fastest.
Arguments:
- jac_blocks: bfloat16 [6144, 6, 128, 128], P(('dom', 'sub')), may hold values from -0.06717514 to 0.06717514
- block_cols: int32 [6144, 6], P(('dom', 'sub')), may hold values from 0 to 19, as said below
- precond: float32 [6144, 36, 128], P(('dom', 'sub')), may hold values from -0.3 to 0.3
- right_side: float32 [6144, 48, 128], P(('dom', 'sub')), may hold values from -6 to 6
- halo_rows: int32 [2048, 2], P(('dom', 'sub')), may hold values from 0 to 11
- surface_tile: int32 [4096], P(('dom', 'sub')), may hold values from 0 to 11
- surface_block: int32 [4096], P(('dom', 'sub')), may hold values from 0 to 31
- surface_count: int32 [512], P(('dom', 'sub')), may hold values from 0 to 8, as said below
- surface_residual_derivative: float32 [4096, 18, 128], P(('dom', 'sub')), may hold values from -6 to 6
- lattice_bernstein_weights: bfloat16 [4096, 128, 128], P(('dom', 'sub')), may hold values from 0 to 0.03125
Outputs:
- adjoint: float32 [6144, 48, 128], P(('dom', 'sub'))
- design_grad: float32 [2, 32, 24, 128], P(None, 'sub')
The draws below stay inside these ranges and needn't reach their ends.
Inputs may be any that keep to these rules, and one draw needn't show every extreme that they name: `block_cols`: entries below 12 name the partition's own tiles; entry 12 + k * 2 + h names halo tile h of neighbour k. `surface_count`: slots at and beyond the count are empty; some partition has all 8 slots live.
All inputs are finite; a program needn't handle non-finite values.
Results may differ from the reference program's by a relative error of at most 0.0055.
Values may be sent and summed in bfloat16 or wider, within the bound.
No kernel may reach another device: no remote copies, remote signals or barrier semaphores. Data moves between devices by JAX's collectives and lax.ppermute only.
A program may use at most 64 MiB of HBM per device.

```python
import jax
import jax.numpy as jnp
from jax import lax

NOBJ = 8
NVAR = 6
TILE_CELL_COUNT = 128
CONTROL_PER_BOX = 128
NB = 6
NEIGH = 4
HALO = 2
TILES_DEV = 12
SURF_DEV = 8
FB_DEV = 4
OUTER = 2
INNER = 5
PARTITIONS = 512
TILES = 6144
SURFACE_SLOTS = 4096
NFB = 32
N_DOM = 64
N_SUB = 8


def draw_jac_blocks(key, part):
    spread = 0.25 * TILE_CELL_COUNT ** (-0.5)
    values = jnp.clip(jax.random.normal(key, (TILES, NB, TILE_CELL_COUNT, TILE_CELL_COUNT), jnp.float32), -3.0, 3.0)
    return (values * spread).astype(jnp.bfloat16)


def draw_precond(key, part):
    values = jnp.clip(jax.random.normal(key, (TILES, NVAR * NVAR, TILE_CELL_COUNT), jnp.float32), -3.0, 3.0)
    return values * 0.1


def draw_block_cols(key, part):
    random_cols = jax.random.randint(key, (TILES, NB - 1), 0, TILES_DEV + NEIGH * HALO)
    local_index = jnp.arange(TILES, dtype=jnp.int32) % TILES_DEV
    forced = TILES_DEV + local_index % (NEIGH * HALO)
    return jnp.concatenate([random_cols.astype(jnp.int32), forced[:, None].astype(jnp.int32)], axis=1)


def draw_surface_count(key, part):
    first_key, second_key, third_key = jax.random.split(key, 3)
    blade = jax.random.randint(first_key, (PARTITIONS,), 0, 4) == 0
    farfield = jax.random.randint(second_key, (PARTITIONS,), 0, SURF_DEV // 4 + 1)
    counts = jnp.where(blade, SURF_DEV, farfield).astype(jnp.int32)
    chosen = jax.random.randint(third_key, (), 0, PARTITIONS)
    return counts.at[chosen].set(SURF_DEV)


def with_ends(values, rng, low, top_value):
    spot = [jax.random.randint(jax.random.fold_in(rng, axis), (), 0, length) for axis, length in enumerate(values.shape)]
    main_axis = values.shape.index(max(values.shape))
    next_to = spot[:main_axis] + [(spot[main_axis] + 1) % values.shape[main_axis]] + spot[main_axis + 1:]
    return values.at[tuple(spot)].set(low).at[tuple(next_to)].set(top_value)


def level_of(key, extent, shards, low, largest):
    loudness, own = 1.0, jax.random.fold_in(key, 6)
    for dim, shards_of in shards:
        steps = jnp.exp(jax.random.uniform(jax.random.fold_in(own, dim), (shards_of,), jnp.float32, low / len(shards), largest / len(shards)))
        loudness = loudness * jnp.repeat(steps, extent[dim] // shards_of).reshape([-1 if axis == dim else 1 for axis in range(len(extent))])
    return loudness


def noise(rng, extent, width, bound, cuts=(), kind=jnp.bfloat16):
    entries = jax.random.normal(rng, extent, jnp.float32) * width
    if len(cuts) > 0:
        entries = level_of(rng, extent, cuts, -0.22, 0.18) * entries
    return jnp.clip(entries, min=-bound, max=bound).astype(kind)


def setup_inputs(seed: int = 0) -> dict:
    keys = jax.random.split(jax.random.key(seed), 11)
    jac_blocks = draw_jac_blocks(jax.random.fold_in(keys[10], 71), 0)
    block_cols = draw_block_cols(jax.random.fold_in(keys[10], 71), 0)
    precond = draw_precond(jax.random.fold_in(keys[10], 71), 0)
    right_side = noise(keys[3], (TILES, NOBJ * NVAR, TILE_CELL_COUNT), 1.0, 6.0, ((0, 512),), jnp.float32)
    halo_rows = with_ends(jax.random.randint(keys[4], (PARTITIONS * NEIGH, HALO), 0, TILES_DEV), jax.random.fold_in(keys[4], 1), 0, TILES_DEV - 1).astype(jnp.int32)
    surface_tile = with_ends(jax.random.randint(keys[5], (SURFACE_SLOTS,), 0, TILES_DEV), jax.random.fold_in(keys[5], 1), 0, TILES_DEV - 1).astype(jnp.int32)
    surface_block = with_ends(jax.random.randint(keys[6], (SURFACE_SLOTS,), 0, NFB), jax.random.fold_in(keys[6], 1), 0, NFB - 1).astype(jnp.int32)
    surface_count = draw_surface_count(jax.random.fold_in(keys[10], 71), 0)
    surface_residual_derivative = noise(keys[8], (SURFACE_SLOTS, NVAR * 3, TILE_CELL_COUNT), 1.0, 6.0, ((0, 512),), jnp.float32)
    lattice_bernstein_weights = jnp.clip(0.03125 * jax.random.uniform(keys[9], (SURFACE_SLOTS, CONTROL_PER_BOX, TILE_CELL_COUNT), jnp.float32) ** level_of(keys[9], (SURFACE_SLOTS, CONTROL_PER_BOX, TILE_CELL_COUNT), ((0, 512),), -0.2, 0.2), 0.0, 0.03125).astype(jnp.bfloat16)
    return {"jac_blocks": jac_blocks, "block_cols": block_cols, "precond": precond, "right_side": right_side, "halo_rows": halo_rows, "surface_tile": surface_tile, "surface_block": surface_block, "surface_count": surface_count, "surface_residual_derivative": surface_residual_derivative, "lattice_bernstein_weights": lattice_bernstein_weights}


OFFSETS = (1, -1, 2, -2)
RELAXATION = 0.7


def variable_mix(blending_factor, residual):
    tile_count = residual.shape[0]
    cell_count = residual.shape[-1]
    residual_split = residual.reshape(tile_count, NOBJ, NVAR, cell_count)
    mixing_split = blending_factor.reshape(tile_count, NVAR, NVAR, cell_count)
    mixed = jnp.sum(mixing_split[:, None, :, :, :] * residual_split[:, :, None, :, :], axis=3)
    return mixed.reshape(tile_count, NOBJ * NVAR, cell_count)


def pick_columns(extended, columns):
    return extended[columns]


def design_gradient(adjoint_flat, surface_tile, surface_block, surface_count, surface_residual_derivative, lattice_bernstein_weights, scaling):
    slot_count = surface_tile.shape[0]
    owner = jnp.arange(slot_count, dtype=jnp.int32) // SURF_DEV
    selected = adjoint_flat[owner * TILES_DEV + surface_tile]
    weights_split = surface_residual_derivative.reshape(slot_count, 1, NVAR, 3, TILE_CELL_COUNT)
    sensitivity = jnp.sum(selected.reshape(slot_count, NOBJ, NVAR, 1, TILE_CELL_COUNT) * weights_split, axis=2)
    alive = (jnp.arange(SURF_DEV, dtype=jnp.int32)[None, :] < surface_count[:, None]).reshape(slot_count)
    alive = alive.astype(jnp.float32)
    rounded = (sensitivity * alive[:, None, None, None]).reshape(slot_count, NOBJ * 3, TILE_CELL_COUNT).astype(jnp.bfloat16)
    projected = jnp.einsum("uoc,upc->uop", rounded.astype(jnp.float32), lattice_bernstein_weights.astype(jnp.float32))
    summed = jax.ops.segment_sum(projected, surface_block, num_segments=FB_DEV * N_SUB)
    return summed * scaling


def reference(jac_blocks, block_cols, precond, right_side, halo_rows, surface_tile, surface_block, surface_count, surface_residual_derivative, lattice_bernstein_weights):
    partitions = N_DOM * N_SUB
    row_count = NOBJ * NVAR
    blocks = jac_blocks.reshape(partitions, TILES_DEV, NB, TILE_CELL_COUNT, TILE_CELL_COUNT)
    columns = block_cols.reshape(partitions, TILES_DEV, NB)
    blending_factor = precond.reshape(partitions, TILES_DEV, NVAR * NVAR, TILE_CELL_COUNT)
    targets = right_side.reshape(partitions, TILES_DEV, row_count, TILE_CELL_COUNT)
    demanded_items = halo_rows.reshape(partitions, len(OFFSETS), HALO)
    device_ids = jnp.arange(partitions, dtype=jnp.int32)
    group = device_ids // N_SUB
    member = device_ids % N_SUB
    offset_table = jnp.array(OFFSETS, dtype=jnp.int32)
    source = ((group[:, None] - offset_table[None, :]) % N_DOM) * N_SUB + member[:, None]
    halo_global = (source[:, :, None] * TILES_DEV + demanded_items).reshape(partitions, len(OFFSETS) * HALO)
    local_global = device_ids[:, None] * TILES_DEV + jnp.arange(TILES_DEV, dtype=jnp.int32)[None, :]
    extended_global = jnp.concatenate([local_global, halo_global], axis=1).astype(jnp.int32)
    column_global = jax.vmap(pick_columns)(extended_global, columns)
    adjoint = jnp.zeros((partitions, TILES_DEV, row_count, TILE_CELL_COUNT), jnp.float32)
    scaling = (FB_DEV / (SURF_DEV * N_DOM)) ** 0.5
    gradients = []
    for outer_index in range(OUTER):
        for sweep_index in range(INNER):
            rounded = adjoint.astype(jnp.bfloat16).reshape(partitions * TILES_DEV, row_count, TILE_CELL_COUNT)

            def device_sweep(packed):
                block_set, column_set, current, target, mixing_set = packed
                picked = rounded[column_set].astype(jnp.float32)
                coupled = current + jnp.einsum("tbor,tbrc->toc", picked, block_set.astype(jnp.float32))
                residual = target - coupled
                return current + RELAXATION * residual + variable_mix(mixing_set, residual)

            adjoint = lax.map(device_sweep, (blocks, column_global, adjoint, targets, blending_factor))
        adjoint_flat = adjoint.reshape(partitions * TILES_DEV, row_count, TILE_CELL_COUNT)
        gradients.append(design_gradient(adjoint_flat, surface_tile, surface_block, surface_count, surface_residual_derivative, lattice_bernstein_weights, scaling))
    return adjoint.reshape(partitions * TILES_DEV, row_count, TILE_CELL_COUNT), jnp.stack(gradients, axis=0)
```

```python
import functools
import math

import jax
import jax.numpy as jnp
from jax import lax
from jax.experimental import pallas as pl
from jax.experimental.pallas import tpu as pltpu
from jax.sharding import PartitionSpec as P

NOBJ = 8
NVAR = 6
NDIR = 3
FB_DEV = 4
OUTER = 2
INNER = 5
HALO = 2
LINE = 4

OFFSETS = (1, -1, 2, -2)
RELAXATION = 0.7
VMEM = pltpu.MemorySpace.VMEM
SMEM = pltpu.MemorySpace.SMEM
GRANT = pltpu.CompilerParams(vmem_limit_bytes=16 * 1024 * 1024)


def from_behind(value, axis, steps):
    count = lax.axis_size(axis)
    pairs = [(source, (source + steps) % count) for source in range(count)]
    return lax.ppermute(value, axis, pairs)


def relaxed(current, residual, mixing_ref, tile):
    rows = [residual[w * NOBJ : (w + 1) * NOBJ, :] for w in range(NVAR)]
    pieces = []
    for v in range(NVAR):
        total = RELAXATION * rows[v]
        for w in range(NVAR):
            k = v * NVAR + w
            total = total + mixing_ref[tile, k : k + 1, :] * rows[w]
        pieces.append(total)
    update = jnp.concatenate(pieces, axis=0)
    return update if current is None else current + update


def first_kernel(rows_ref, target_ref, mixing_ref, sorted_ref, state_ref, rounded_ref, *payload_refs):
    tiles = target_ref.shape[0]
    for tile in range(tiles):
        target = jnp.concatenate(
            [target_ref[tile, pl.ds(v, NOBJ, stride=NVAR), :] for v in range(NVAR)], axis=0
        )
        sorted_ref[tile] = target
        state = relaxed(None, target, mixing_ref, tile)
        state_ref[tile] = state
        rounded = state.astype(jnp.bfloat16)
        rounded_ref[tile] = rounded
        for payload_ref in payload_refs:
            payload_ref[tile] = rounded
    shape = payload_refs[0].shape[1:]
    half = lax.broadcasted_iota(jnp.int32, shape, 0) < shape[0] // HALO
    for k, payload_ref in enumerate(payload_refs):
        first = rows_ref[k * HALO].astype(jnp.float32)
        second = rows_ref[k * HALO + 1].astype(jnp.float32)
        payload_ref[tiles] = jnp.where(half, first, second).astype(jnp.bfloat16)


def update_tiles(cols_ref, state_ref, extended_ref, target_ref, mixing_ref, blocks_ref, store):
    block_count = blocks_ref.shape[1]
    cells = blocks_ref.shape[3]
    for tile in range(state_ref.shape[0]):
        picked = jnp.concatenate(
            [extended_ref[cols_ref[tile * block_count + b]] for b in range(block_count)], axis=1
        )
        product = jnp.dot(
            picked,
            blocks_ref[tile].reshape(block_count * cells, cells),
            preferred_element_type=jnp.float32,
        )
        current = state_ref[tile]
        residual = target_ref[tile] - (current + product)
        store(tile, relaxed(current, residual, mixing_ref, tile))


def pack(place, needs, rounded_ref, own_ref, layer_ref):
    rows = rounded_ref.shape[1]

    def wanted(offset, h):
        index = jnp.int32(0)
        for k, o in enumerate(OFFSETS):
            index = jnp.where(offset == o, needs[k * HALO + h], index)
        return index

    for h in range(HALO):
        span = slice(h * rows, (h + 1) * rows)
        for peer in range(LINE):
            own_ref[peer, span, :] = rounded_ref[wanted(peer - place, h)]
        for side in range(2):
            there = jnp.where(place < 2, side - 2, side + LINE)
            layer_ref[side, span, :] = rounded_ref[wanted(there - place, h)]


def second_kernel(
    place_ref,
    cols_ref,
    rows_ref,
    state_ref,
    rounded_ref,
    from0_ref,
    from1_ref,
    from2_ref,
    from3_ref,
    target_ref,
    mixing_ref,
    blocks_ref,
    new_ref,
    new_rounded_ref,
    own_ref,
    layer_ref,
    needs_ref,
    extended_ref,
):
    tiles = state_ref.shape[0]
    sources = (from0_ref, from1_ref, from2_ref, from3_ref)
    needs = [None] * (len(OFFSETS) * HALO)
    for k, source_ref in enumerate(sources):
        for h in range(HALO):
            entry = k * HALO + h
            extended_ref[tiles + entry] = source_ref[rows_ref[entry]]
            named = source_ref[tiles, h * 24 : h * 24 + 8, :].astype(jnp.float32)
            told = OFFSETS.index(-OFFSETS[k])
            needs[told * HALO + h] = jnp.max(named).astype(jnp.int32)
    for entry, need in enumerate(needs):
        needs_ref[entry] = need
    for tile in range(tiles):
        extended_ref[tile] = rounded_ref[tile]

    def store(tile, state):
        new_ref[tile] = state
        new_rounded_ref[tile] = state.astype(jnp.bfloat16)

    update_tiles(cols_ref, state_ref, extended_ref, target_ref, mixing_ref, blocks_ref, store)
    pack(place_ref[0], needs, new_rounded_ref, own_ref, layer_ref)


def sweep_kernel(
    last,
    place_ref,
    cols_ref,
    needs_ref,
    state_ref,
    rounded_ref,
    halo_ref,
    target_ref,
    mixing_ref,
    blocks_ref,
    new_ref,
    *rest,
):
    tiles = state_ref.shape[0]
    rows = state_ref.shape[1]
    extended_ref = rest[-1]
    place = place_ref[0]
    for k, offset in enumerate(OFFSETS):
        source = place - offset
        relayed = jnp.where((source < 0) | (source >= LINE), 1, 0)
        peer = source & (LINE - 1)
        for h in range(HALO):
            start = pl.multiple_of((relayed * HALO + h) * rows, 16)
            extended_ref[tiles + k * HALO + h] = halo_ref[peer, pl.ds(start, rows), :]
    for tile in range(tiles):
        extended_ref[tile] = rounded_ref[tile]

    def store(tile, state):
        new_ref[tile] = state
        if last:
            for v in range(NVAR):
                part = state[v * NOBJ : (v + 1) * NOBJ, :]
                rest[0][tile, pl.ds(v, NOBJ, stride=NVAR), :] = part
        else:
            rest[0][tile] = state.astype(jnp.bfloat16)

    update_tiles(cols_ref, state_ref, extended_ref, target_ref, mixing_ref, blocks_ref, store)
    if not last:
        needs = [needs_ref[entry] for entry in range(len(OFFSETS) * HALO)]
        pack(place, needs, rest[0], rest[1], rest[2])


def design_kernel(
    tile_ref, block_ref, count_ref, state_ref, derivative_ref, weights_ref, out_ref, sum_ref
):
    owners = sum_ref.shape[0] // 2
    rows = NOBJ * NDIR
    sum_ref[...] = jnp.zeros(sum_ref.shape, jnp.float32)
    for slot in range(weights_ref.shape[0]):
        tile = tile_ref[slot]
        selected = state_ref[tile]
        pieces = []
        for k in range(NDIR):
            total = None
            for v in range(NVAR):
                row = v * NDIR + k
                term = (
                    selected[v * NOBJ : (v + 1) * NOBJ, :]
                    * derivative_ref[slot, row : row + 1, :]
                )
                total = term if total is None else total + term
            pieces.append(total)
        sensitivity = jnp.concatenate(pieces, axis=0)
        alive = slot < count_ref[0]
        sensitivity = jnp.where(alive, sensitivity, 0.0)
        coarse = sensitivity.astype(jnp.bfloat16)
        fine = sensitivity - coarse.astype(jnp.float32)
        halves = lax.dot_general(
            jnp.concatenate([coarse.astype(jnp.float32), fine], axis=0).astype(jnp.bfloat16),
            weights_ref[slot],
            (((1,), (1,)), ((), ())),
            preferred_element_type=jnp.float32,
        )
        projected = halves[:rows] + halves[rows:]
        block = block_ref[slot]
        within = block % FB_DEV
        chunk = (within // 2) * owners + block // FB_DEV
        start = pl.multiple_of((within % 2) * rows, 8)
        sum_ref[chunk, pl.ds(start, rows), :] = sum_ref[chunk, pl.ds(start, rows), :] + projected
    for chunk in range(sum_ref.shape[0]):
        out_ref[chunk] = sum_ref[chunk].astype(jnp.bfloat16)


def vmem(count):
    return [pl.BlockSpec(memory_space=VMEM)] * count


def smem(count):
    return [pl.BlockSpec(memory_space=SMEM)] * count


def first_sweep(rows, target, mixing):
    shape = jax.ShapeDtypeStruct(target.shape, jnp.float32)
    rounded = jax.ShapeDtypeStruct(target.shape, jnp.bfloat16)
    payload = jax.ShapeDtypeStruct((target.shape[0] + 1,) + target.shape[1:], jnp.bfloat16)
    return pl.pallas_call(
        first_kernel,
        out_shape=(shape, shape, rounded) + (payload,) * len(OFFSETS),
        in_specs=smem(1) + vmem(2),
        out_specs=tuple(vmem(3 + len(OFFSETS))),
        compiler_params=GRANT,
        name="first_sweep",
    )(rows, target, mixing)


def sweep_shapes(state):
    chunk = (HALO * state.shape[1], state.shape[2])
    return (
        jax.ShapeDtypeStruct(state.shape, jnp.float32),
        jax.ShapeDtypeStruct(state.shape, jnp.bfloat16),
        jax.ShapeDtypeStruct((LINE,) + chunk, jnp.bfloat16),
        jax.ShapeDtypeStruct((2,) + chunk, jnp.bfloat16),
    )


def extended_scratch(state):
    tiles = state.shape[0] + len(OFFSETS) * HALO
    return [pltpu.VMEM((tiles,) + state.shape[1:], jnp.bfloat16)]


def second_sweep(place, cols, rows, state, rounded, sources, target, mixing, blocks):
    needs = jax.ShapeDtypeStruct((len(OFFSETS) * HALO,), jnp.int32)
    return pl.pallas_call(
        second_kernel,
        out_shape=sweep_shapes(state) + (needs,),
        in_specs=smem(3) + vmem(9),
        out_specs=tuple(vmem(4) + smem(1)),
        scratch_shapes=extended_scratch(state),
        compiler_params=GRANT,
        name="second_sweep",
    )(place, cols, rows, state, rounded, *sources, target, mixing, blocks)


def sweep(place, cols, needs, state, rounded, halo, target, mixing, blocks, last):
    shapes = sweep_shapes(state)
    out_shape = (shapes[0], shapes[0]) if last else shapes
    return pl.pallas_call(
        functools.partial(sweep_kernel, last),
        out_shape=out_shape,
        in_specs=smem(3) + vmem(6),
        out_specs=tuple(vmem(len(out_shape))),
        scratch_shapes=extended_scratch(state),
        compiler_params=GRANT,
        name="last_sweep" if last else "sweep",
    )(place, cols, needs, state, rounded, halo, target, mixing, blocks)


def exchange(own, layer):
    count = lax.axis_size("dom")
    steps = [LINE if source % LINE >= 2 else -LINE for source in range(count)]
    pairs = [(source, (source + step) % count) for source, step in enumerate(steps)]
    relayed = lax.ppermute(layer, "dom", pairs)
    chunks = jnp.concatenate([own, jnp.concatenate([relayed, relayed], axis=0)], axis=1)
    lines = [[start + x for x in range(LINE)] for start in range(0, count, LINE)]
    return lax.all_to_all(chunks, "dom", 0, 0, axis_index_groups=lines)


def design_partial(tile, block, count, state, derivative, weights, owners):
    chunk = (2 * owners, 2 * NOBJ * NDIR, weights.shape[1])
    return pl.pallas_call(
        design_kernel,
        out_shape=jax.ShapeDtypeStruct(chunk, jnp.bfloat16),
        in_specs=smem(3) + vmem(3),
        out_specs=pl.BlockSpec(memory_space=VMEM),
        scratch_shapes=[pltpu.VMEM(chunk, jnp.float32)],
        compiler_params=GRANT,
        name="design_partial",
    )(tile, block, count, state, derivative, weights)


def reduce_design(first, second, scaling):
    dom, sub = lax.axis_size("dom"), lax.axis_size("sub")
    columns = LINE
    layers = dom // columns
    plane = columns * sub
    chunks = jnp.concatenate([first, second], axis=0)
    planes = [[layer * plane + i for i in range(plane)] for layer in range(layers)]
    spread = lax.all_to_all(chunks, ("dom", "sub"), 0, 0, axis_index_groups=planes)
    mine = jnp.sum(spread.astype(jnp.float32), axis=0).astype(jnp.bfloat16)
    stacks = [[layer * columns + x for layer in range(layers)] for x in range(columns)]
    copies = jnp.broadcast_to(mine[None], (layers,) + mine.shape)
    stacked = lax.all_to_all(copies, "dom", 0, 0, axis_index_groups=stacks)
    total = jnp.sum(stacked.astype(jnp.float32), axis=0) * scaling
    lines = [[layer * columns + x for x in range(columns)] for layer in range(layers)]
    copies = jnp.broadcast_to(total[None], (columns,) + total.shape)
    gathered = lax.all_to_all(copies, "dom", 0, 0, axis_index_groups=lines)
    split = gathered.reshape(OUTER, FB_DEV, NDIR, NOBJ, gathered.shape[-1])
    return split.swapaxes(2, 3).reshape(OUTER, FB_DEV, NOBJ * NDIR, gathered.shape[-1])


def per_device(
    jac_blocks,
    block_cols,
    precond,
    right_side,
    halo_rows,
    surface_tile,
    surface_block,
    surface_count,
    surface_residual_derivative,
    lattice_bernstein_weights,
):
    slot_count = surface_tile.shape[0]
    scaling = math.sqrt(FB_DEV / (slot_count * lax.axis_size("dom")))
    cols = block_cols.reshape(-1)
    rows = halo_rows.reshape(-1)
    place = (lax.axis_index("dom") % LINE).astype(jnp.int32).reshape(1)
    target, state, rounded, *payloads = first_sweep(rows, right_side, precond)
    partials = []
    adjoint = None
    for outer_index in range(OUTER):
        for sweep_index in range(INNER):
            number = outer_index * INNER + sweep_index
            last = number == OUTER * INNER - 1
            if number == 0:
                continue
            if number == 1:
                sources = [
                    from_behind(payloads[OFFSETS.index(-offset)], "dom", offset)
                    for offset in OFFSETS
                ]
                state, rounded, own, layer, needs = second_sweep(
                    place, cols, rows, state, rounded, sources, target, precond, jac_blocks
                )
                continue
            halo = exchange(own, layer)
            result = sweep(
                place, cols, needs, state, rounded, halo, target, precond, jac_blocks, last
            )
            if last:
                state, adjoint = result
            else:
                state, rounded, own, layer = result
        partials.append(
            design_partial(
                surface_tile,
                surface_block,
                surface_count,
                state,
                surface_residual_derivative,
                lattice_bernstein_weights,
                lax.axis_size("sub"),
            )
        )
    return (adjoint, reduce_design(partials[0], partials[1], scaling))


def solution(mesh):
    in_specs = (
        P(("dom", "sub"), None, None, None),
        P(("dom", "sub"), None),
        P(("dom", "sub"), None, None),
        P(("dom", "sub"), None, None),
        P(("dom", "sub"), None),
        P(("dom", "sub")),
        P(("dom", "sub")),
        P(("dom", "sub")),
        P(("dom", "sub"), None, None),
        P(("dom", "sub"), None, None),
    )
    out_specs = (P(("dom", "sub"), None, None), P(None, "sub", None, None))
    return jax.shard_map(
        per_device, mesh=mesh, in_specs=in_specs, out_specs=out_specs, check_vma=False
    )
```

```python
import functools
import math

import jax
import jax.numpy as jnp
from jax import lax
from jax.experimental import pallas as pl
from jax.experimental.pallas import tpu as pltpu
from jax.sharding import PartitionSpec as P

NOBJ = 8
NVAR = 6
NDIR = 3
FB_DEV = 4
OUTER = 2
INNER = 5
HALO = 2
LINE = 4

OFFSETS = (1, -1, 2, -2)
NEEDS = len(OFFSETS) * HALO
COLS = 32
PLACE = COLS - 1
PART = 3
RELAXATION = 0.7
VMEM = pltpu.MemorySpace.VMEM
SMEM = pltpu.MemorySpace.SMEM
HBM = pltpu.MemorySpace.HBM
GRANT = pltpu.CompilerParams(vmem_limit_bytes=16 * 1024 * 1024)


def specs(*kinds):
    return [pl.BlockSpec(memory_space=kind) for kind in kinds]


def from_behind(value, axis, steps):
    count = lax.axis_size(axis)
    pairs = [(source, (source + steps) % count) for source in range(count)]
    return lax.ppermute(value, axis, pairs)


def relaxed(current, residual, mixing_ref, tile):
    rows = [residual[w * NOBJ : (w + 1) * NOBJ, :] for w in range(NVAR)]
    pieces = []
    for v in range(NVAR):
        total = RELAXATION * rows[v]
        for w in range(NVAR):
            k = v * NVAR + w
            total = total + mixing_ref[tile, k : k + 1, :] * rows[w]
        pieces.append(total)
    update = jnp.concatenate(pieces, axis=0)
    return update if current is None else current + update


def first_kernel(
    rows_hbm,
    target_hbm,
    mixing_hbm,
    sorted_ref,
    state_ref,
    payload_ref,
    rows_ref,
    target_ref,
    mixing_ref,
    sems,
):
    pairs = ((target_hbm, target_ref), (mixing_hbm, mixing_ref), (rows_hbm, rows_ref))
    copies = [pltpu.make_async_copy(*pair, sems.at[i]) for i, pair in enumerate(pairs)]
    for copy in copies:
        copy.start()
    for copy in copies:
        copy.wait()
    tiles = target_ref.shape[0]
    for tile in range(tiles):
        target = jnp.concatenate(
            [target_ref[tile, pl.ds(v, NOBJ, stride=NVAR), :] for v in range(NVAR)], axis=0
        )
        sorted_ref[tile] = target
        state = relaxed(None, target, mixing_ref, tile)
        state_ref[tile] = state
        payload_ref[tile] = state.astype(jnp.bfloat16)
    row = lax.broadcasted_iota(jnp.int32, payload_ref.shape[1:], 0)
    told = jnp.zeros(payload_ref.shape[1:], jnp.float32)
    for k in range(len(OFFSETS)):
        for h in range(HALO):
            told = jnp.where(row == k * HALO + h, rows_ref[h, k].astype(jnp.float32), told)
    payload_ref[tiles] = told.astype(jnp.bfloat16)


def update_tiles(
    table_ref, state_ref, extended_ref, target_ref, mixing_ref, blocks_ref, store, before=None
):
    block_count = blocks_ref.shape[1]
    cells = blocks_ref.shape[3]
    for tile in range(state_ref.shape[0]):
        if before is not None:
            before(tile)
        first = COLS + tile * block_count
        picked = jnp.concatenate(
            [extended_ref[table_ref[first + b]] for b in range(block_count)], axis=1
        )
        product = jnp.dot(
            picked,
            blocks_ref[tile].reshape(block_count * cells, cells),
            preferred_element_type=jnp.float32,
        )
        current = state_ref[tile]
        residual = target_ref[tile] - (current + product)
        store(tile, relaxed(current, residual, mixing_ref, tile))


def pack(place, needs, rounded_ref, own_ref, layer_ref):
    rows = rounded_ref.shape[1]

    def wanted(offset, h):
        index = jnp.int32(0)
        for k, o in enumerate(OFFSETS):
            index = jnp.where(offset == o, needs[k * HALO + h], index)
        return index

    for h in range(HALO):
        span = slice(h * rows, (h + 1) * rows)
        for peer in range(LINE):
            own_ref[peer, span, :] = rounded_ref[wanted(peer - place, h)]
        for side in range(2):
            there = jnp.where(place < 2, side - 2, side + LINE)
            layer_ref[side, span, :] = rounded_ref[wanted(there - place, h)]


def second_kernel(
    cols_hbm,
    rows_hbm,
    tile_hbm,
    block_hbm,
    mixing_hbm,
    blocks_hbm,
    count_ref,
    place_ref,
    state_ref,
    rounded_ref,
    from0_ref,
    from1_ref,
    from2_ref,
    from3_ref,
    target_ref,
    new_ref,
    new_rounded_ref,
    own_ref,
    layer_ref,
    table_ref,
    cols_ref,
    rows_ref,
    tile_ref,
    block_ref,
    mixing_ref,
    blocks_ref,
    extended_ref,
    told_ref,
    sems,
):
    tiles = state_ref.shape[0]
    small = (
        (rows_hbm, rows_ref),
        (cols_hbm, cols_ref),
        (tile_hbm, tile_ref),
        (block_hbm, block_ref),
    )
    number = iter(range(sems.shape[0]))
    first = [pltpu.make_async_copy(*pair, sems.at[next(number)]) for pair in small]
    large = [pltpu.make_async_copy(mixing_hbm, mixing_ref, sems.at[next(number)])]
    parts = []
    for start in range(0, tiles, PART):
        span = pl.ds(start, PART)
        parts.append(
            pltpu.make_async_copy(
                blocks_hbm.at[span], blocks_ref.at[span], sems.at[next(number)]
            )
        )
    for copy in first + large + parts:
        copy.start()
    for tile in range(tiles):
        extended_ref[tile] = rounded_ref[tile]
    for copy in first:
        copy.wait()
    sources = (from0_ref, from1_ref, from2_ref, from3_ref)
    copies = []
    for k, source_ref in enumerate(sources):
        for h in range(HALO):
            copies.append(
                pltpu.make_async_copy(
                    source_ref.at[rows_ref[h, k]],
                    extended_ref.at[tiles + k * HALO + h],
                    sems.at[next(number)],
                )
            )
        copies.append(
            pltpu.make_async_copy(source_ref.at[tiles], told_ref.at[k], sems.at[next(number)])
        )
    for copy in copies:
        copy.start()
    block_count = blocks_ref.shape[1]
    for tile in range(tiles):
        for b in range(block_count):
            table_ref[COLS + tile * block_count + b] = cols_ref[b, tile]
    slots = tile_ref.shape[0]
    for slot in range(slots):
        table_ref[NEEDS + slot] = tile_ref[slot]
        table_ref[NEEDS + slots + slot] = block_ref[slot]
    table_ref[NEEDS + 2 * slots] = count_ref[0]
    place = place_ref[0]
    table_ref[PLACE] = place
    for copy in copies:
        copy.wait()
    needs = [None] * NEEDS
    for k in range(len(sources)):
        named = told_ref[k].astype(jnp.float32)
        row = lax.broadcasted_iota(jnp.int32, named.shape, 0)
        told = OFFSETS.index(-OFFSETS[k])
        for h in range(HALO):
            entry = told * HALO + h
            needs[entry] = jnp.max(jnp.where(row == entry, named, 0.0)).astype(jnp.int32)
    for entry, need in enumerate(needs):
        table_ref[entry] = need
    for copy in large:
        copy.wait()

    def before(tile):
        if tile % PART == 0:
            parts[tile // PART].wait()

    def store(tile, state):
        new_ref[tile] = state
        new_rounded_ref[tile] = state.astype(jnp.bfloat16)

    update_tiles(
        table_ref, state_ref, extended_ref, target_ref, mixing_ref, blocks_ref, store, before
    )
    pack(place, needs, new_rounded_ref, own_ref, layer_ref)


def design_sum(table_ref, state_ref, derivative_ref, weights_ref, sum_ref):
    owners = sum_ref.shape[0] // FB_DEV
    rows = NOBJ * NDIR
    slots = weights_ref.shape[0]
    sum_ref[...] = jnp.zeros(sum_ref.shape, jnp.float32)
    for slot in range(slots):
        selected = state_ref[table_ref[NEEDS + slot]]
        pieces = []
        for k in range(NDIR):
            total = None
            for v in range(NVAR):
                term = (
                    selected[v * NOBJ : (v + 1) * NOBJ, :]
                    * derivative_ref[v * NDIR + k, slot : slot + 1, :]
                )
                total = term if total is None else total + term
            pieces.append(total)
        alive = slot < table_ref[NEEDS + 2 * slots]
        sensitivity = jnp.where(alive, jnp.concatenate(pieces, axis=0), 0.0)
        coarse = sensitivity.astype(jnp.bfloat16).astype(jnp.float32)
        halves = lax.dot_general(
            jnp.concatenate([coarse, sensitivity - coarse], axis=0).astype(jnp.bfloat16),
            weights_ref[slot],
            (((1,), (1,)), ((), ())),
            preferred_element_type=jnp.float32,
        )
        block = table_ref[NEEDS + slots + slot]
        chunk = (block % FB_DEV) * owners + block // FB_DEV
        sum_ref[chunk] = sum_ref[chunk] + (halves[:rows] + halves[rows:])


def sweep_kernel(kind, *refs):
    table_ref, state_ref, rounded_ref, halo_ref, target_ref, mixing_ref, blocks_ref = refs[:7]
    refs = list(refs[7:])
    copies = []
    if kind != "middle":
        derivative_hbm, weights_hbm = refs[:2]
        refs = refs[2:]
        sems = refs.pop()
        sum_ref, weights_ref, derivative_ref = refs.pop(), refs.pop(), refs.pop()
        copies.append(pltpu.make_async_copy(derivative_hbm, derivative_ref, sems.at[0]))
        copies.append(pltpu.make_async_copy(weights_hbm, weights_ref, sems.at[1]))
    extended_ref = refs.pop()
    if kind == "last":
        earlier_hbm, adjoint_hbm, chunks_ref = refs[:3]
        new_ref, adjoint_ref = refs[3:]
        half = sum_ref.shape[0]
        copies.append(
            pltpu.make_async_copy(earlier_hbm, chunks_ref.at[pl.ds(0, half)], sems.at[2])
        )
    elif kind == "design":
        partial_hbm, new_ref, new_rounded_ref, own_ref, layer_ref, partial_ref = refs
    else:
        new_ref, new_rounded_ref, own_ref, layer_ref = refs
    for copy in copies:
        copy.start()
    tiles = state_ref.shape[0]
    rows = state_ref.shape[1]
    place = table_ref[PLACE]
    for k, offset in enumerate(OFFSETS):
        source = place - offset
        relayed = jnp.where((source < 0) | (source >= LINE), 1, 0)
        peer = source & (LINE - 1)
        for h in range(HALO):
            start = pl.multiple_of((relayed * HALO + h) * rows, 16)
            extended_ref[tiles + k * HALO + h] = halo_ref[peer, pl.ds(start, rows), :]
    for tile in range(tiles):
        extended_ref[tile] = rounded_ref[tile]

    def store(tile, state):
        new_ref[tile] = state
        if kind == "last":
            for v in range(NVAR):
                part = state[v * NOBJ : (v + 1) * NOBJ, :]
                adjoint_ref[tile, pl.ds(v, NOBJ, stride=NVAR), :] = part
        else:
            new_rounded_ref[tile] = state.astype(jnp.bfloat16)

    update_tiles(table_ref, state_ref, extended_ref, target_ref, mixing_ref, blocks_ref, store)
    if kind == "last":
        written = pltpu.make_async_copy(adjoint_ref, adjoint_hbm, sems.at[3])
        written.start()
    if kind != "middle":
        for copy in copies:
            copy.wait()
        design_sum(table_ref, new_ref, derivative_ref, weights_ref, sum_ref)
    if kind == "design":
        partial_ref[...] = sum_ref[...].astype(jnp.bfloat16)
        written = pltpu.make_async_copy(partial_ref, partial_hbm, sems.at[2])
        written.start()
    if kind == "last":
        chunks_ref[pl.ds(half, half)] = sum_ref[...].astype(jnp.bfloat16)
    else:
        needs = [table_ref[entry] for entry in range(NEEDS)]
        pack(place, needs, new_rounded_ref, own_ref, layer_ref)
    if kind != "middle":
        written.wait()


def in_hbm(value):
    return pltpu.with_memory_space_constraint(value, HBM)


def first_sweep(rows, target, mixing):
    shape = jax.ShapeDtypeStruct(target.shape, jnp.float32)
    payload = jax.ShapeDtypeStruct((target.shape[0] + 1,) + target.shape[1:], jnp.bfloat16)
    return pl.pallas_call(
        first_kernel,
        out_shape=(shape, shape, payload),
        in_specs=specs(HBM, HBM, HBM),
        out_specs=tuple(specs(VMEM, VMEM, VMEM)),
        scratch_shapes=[
            pltpu.SMEM(rows.shape, rows.dtype),
            pltpu.VMEM(target.shape, target.dtype),
            pltpu.VMEM(mixing.shape, mixing.dtype),
            pltpu.SemaphoreType.DMA((3,)),
        ],
        compiler_params=GRANT,
        name="first_sweep",
    )(in_hbm(rows), in_hbm(target), in_hbm(mixing))


def sweep_shapes(state):
    chunk = (HALO * state.shape[1], state.shape[2])
    return (
        jax.ShapeDtypeStruct(state.shape, jnp.float32),
        jax.ShapeDtypeStruct(state.shape, jnp.bfloat16),
        jax.ShapeDtypeStruct((LINE,) + chunk, jnp.bfloat16),
        jax.ShapeDtypeStruct((2,) + chunk, jnp.bfloat16),
    )


def extended_scratch(state):
    return pltpu.VMEM((state.shape[0] + NEEDS,) + state.shape[1:], jnp.bfloat16)


def second_sweep(place, cols, rows, indices, state, payload, sources, target, mixing, blocks):
    table = jax.ShapeDtypeStruct((COLS + cols.size,), jnp.int32)
    small = (cols, rows) + indices[:2]
    kept = [in_hbm(value) for value in small + (mixing, blocks)]
    own = [pltpu.SMEM(value.shape, value.dtype) for value in small]
    own += [pltpu.VMEM(value.shape, value.dtype) for value in (mixing, blocks)]
    tiles = state.shape[0]
    copies = len(own) - 1 + tiles // PART + NEEDS + len(OFFSETS)
    return pl.pallas_call(
        second_kernel,
        out_shape=sweep_shapes(state) + (table,),
        in_specs=specs(*[HBM] * 6, SMEM, SMEM, VMEM, VMEM, *[pl.ANY] * 4, VMEM),
        out_specs=tuple(specs(VMEM, VMEM, VMEM, VMEM, SMEM)),
        scratch_shapes=own
        + [
            extended_scratch(state),
            pltpu.VMEM((len(OFFSETS),) + state.shape[1:], jnp.bfloat16),
            pltpu.SemaphoreType.DMA((copies,)),
        ],
        compiler_params=GRANT,
        name="second_sweep",
    )(*kept, indices[2], place, state, payload, *sources, target)


def sweep(kind, table, state, rounded, halo, target, mixing, blocks, design=()):
    shapes = sweep_shapes(state)
    scratch = [extended_scratch(state)]
    in_specs = specs(SMEM, VMEM, VMEM, VMEM, VMEM, VMEM, VMEM)
    out_specs = specs(VMEM, VMEM, VMEM, VMEM)
    if kind != "middle":
        derivative, weights = design[:2]
        design = [in_hbm(value) for value in design]
        sums = (FB_DEV * lax.axis_size("sub"), NOBJ * NDIR, weights.shape[1])
        extra = [
            pltpu.VMEM(derivative.shape, derivative.dtype),
            pltpu.VMEM(weights.shape, weights.dtype),
            pltpu.VMEM(sums, jnp.float32),
            pltpu.SemaphoreType.DMA((4,)),
        ]
        in_specs += specs(HBM, HBM)
    if kind == "last":
        in_specs += specs(HBM)
        chunks = jax.ShapeDtypeStruct((OUTER * sums[0],) + sums[1:], jnp.bfloat16)
        shapes = (shapes[0], chunks)
        out_specs = specs(HBM, VMEM)
        full = pltpu.VMEM(state.shape, jnp.float32)
        scratch = [full, full] + scratch + extra
    elif kind == "design":
        shapes = (HBM(sums, jnp.bfloat16),) + shapes
        out_specs = specs(HBM) + out_specs
        scratch = [pltpu.VMEM(sums, jnp.bfloat16)] + scratch + extra
    return pl.pallas_call(
        functools.partial(sweep_kernel, kind),
        out_shape=shapes,
        in_specs=in_specs,
        out_specs=tuple(out_specs),
        scratch_shapes=scratch,
        compiler_params=GRANT,
        name="sweep_" + kind,
    )(table, state, rounded, halo, target, mixing, blocks, *design)


def exchange(own, layer):
    count = lax.axis_size("dom")
    steps = [LINE if source % LINE >= 2 else -LINE for source in range(count)]
    pairs = [(source, (source + step) % count) for source, step in enumerate(steps)]
    relayed = lax.ppermute(layer, "dom", pairs)
    chunks = jnp.concatenate([own, jnp.concatenate([relayed, relayed], axis=0)], axis=1)
    lines = [[start + x for x in range(LINE)] for start in range(0, count, LINE)]
    return lax.all_to_all(chunks, "dom", 0, 0, axis_index_groups=lines)


def reduce_design(chunks, scaling):
    dom, sub = lax.axis_size("dom"), lax.axis_size("sub")
    part = OUTER * FB_DEV
    slabs = dom // part
    wide = part * sub
    groups = [[slab * wide + i for i in range(wide)] for slab in range(slabs)]
    spread = lax.all_to_all(chunks, ("dom", "sub"), 0, 0, axis_index_groups=groups)
    mine = jnp.sum(spread.astype(jnp.float32), axis=0)
    groups = [[slab * part + i for slab in range(slabs)] for i in range(part)]
    copies = jnp.broadcast_to(mine[None], (slabs,) + mine.shape)
    stacked = lax.all_to_all(copies, "dom", 0, 0, axis_index_groups=groups)
    total = jnp.sum(stacked, axis=0) * scaling
    groups = [[slab * part + i for i in range(part)] for slab in range(slabs)]
    copies = jnp.broadcast_to(total[None], (part,) + total.shape)
    gathered = lax.all_to_all(copies, "dom", 0, 0, axis_index_groups=groups)
    split = gathered.reshape(OUTER, FB_DEV, NDIR, NOBJ, gathered.shape[-1])
    return split.swapaxes(2, 3).reshape(OUTER, FB_DEV, NOBJ * NDIR, gathered.shape[-1])


def per_device(
    jac_blocks,
    block_cols,
    precond,
    right_side,
    halo_rows,
    surface_tile,
    surface_block,
    surface_count,
    surface_residual_derivative,
    lattice_bernstein_weights,
):
    slot_count = surface_tile.shape[0]
    scaling = math.sqrt(FB_DEV / (slot_count * lax.axis_size("dom")))
    cols = block_cols.T
    rows = halo_rows.T
    place = (lax.axis_index("dom") % LINE).astype(jnp.int32).reshape(1)
    indices = (surface_tile, surface_block, surface_count)
    design = (surface_residual_derivative.transpose(1, 0, 2), lattice_bernstein_weights)
    target, state, payload = first_sweep(rows, right_side, precond)
    sources = [from_behind(payload, "dom", offset) for offset in OFFSETS]
    state, rounded, own, layer, table = second_sweep(
        place, cols, rows, indices, state, payload, sources, target, precond, jac_blocks
    )
    count = OUTER * INNER
    for number in range(2, count):
        halo = exchange(own, layer)
        arrays = (table, state, rounded, halo, target, precond, jac_blocks)
        if number == count - 1:
            adjoint, chunks = sweep("last", *arrays, design + (partial,))
        elif number == INNER - 1:
            partial, state, rounded, own, layer = sweep("design", *arrays, design)
        else:
            state, rounded, own, layer = sweep("middle", *arrays)
    return (adjoint, reduce_design(chunks, scaling))


def solution(mesh):
    in_specs = (
        P(("dom", "sub"), None, None, None),
        P(("dom", "sub"), None),
        P(("dom", "sub"), None, None),
        P(("dom", "sub"), None, None),
        P(("dom", "sub"), None),
        P(("dom", "sub")),
        P(("dom", "sub")),
        P(("dom", "sub")),
        P(("dom", "sub"), None, None),
        P(("dom", "sub"), None, None),
    )
    out_specs = (P(("dom", "sub"), None, None), P(None, "sub", None, None))
    return jax.shard_map(
        per_device, mesh=mesh, in_specs=in_specs, out_specs=out_specs, check_vma=False
    )
```

```python
import functools
import math

import jax
import jax.numpy as jnp
from jax import lax
from jax.experimental import pallas as pl
from jax.experimental.pallas import tpu as pltpu
from jax.sharding import PartitionSpec as P

NOBJ = 8
NVAR = 6
NDIR = 3
FB_DEV = 4
OUTER = 2
INNER = 5
HALO = 2
LINE = 4

OFFSETS = (1, -1, 2, -2)
NEEDS = len(OFFSETS) * HALO
COLS = 32
PLACE = COLS - 1
PART = 3
RELAXATION = 0.7
VMEM = pltpu.MemorySpace.VMEM
SMEM = pltpu.MemorySpace.SMEM
HBM = pltpu.MemorySpace.HBM
GRANT = pltpu.CompilerParams(vmem_limit_bytes=16 * 1024 * 1024)


def specs(*kinds):
    return [pl.BlockSpec(memory_space=kind) for kind in kinds]


def from_behind(value, axis, steps):
    count = lax.axis_size(axis)
    pairs = [(source, (source + steps) % count) for source in range(count)]
    return lax.ppermute(value, axis, pairs)


def relaxed(current, residual, mixing_ref, tile):
    rows = [residual[w * NOBJ : (w + 1) * NOBJ, :] for w in range(NVAR)]
    pieces = []
    for v in range(NVAR):
        total = RELAXATION * rows[v]
        for w in range(NVAR):
            k = v * NVAR + w
            total = total + mixing_ref[tile, k : k + 1, :] * rows[w]
        pieces.append(total)
    update = jnp.concatenate(pieces, axis=0)
    return update if current is None else current + update


def first_kernel(
    rows_hbm,
    cols_hbm,
    tile_hbm,
    block_hbm,
    target_hbm,
    mixing_hbm,
    count_ref,
    place_ref,
    sorted_ref,
    state_ref,
    payload_ref,
    table_ref,
    rows_ref,
    cols_ref,
    tile_ref,
    block_ref,
    target_ref,
    mixing_ref,
    sems,
):
    pairs = (
        (target_hbm, target_ref),
        (mixing_hbm, mixing_ref),
        (rows_hbm, rows_ref),
        (cols_hbm, cols_ref),
        (tile_hbm, tile_ref),
        (block_hbm, block_ref),
    )
    copies = [pltpu.make_async_copy(*pair, sems.at[i]) for i, pair in enumerate(pairs)]
    for copy in copies:
        copy.start()
    for copy in copies[2:]:
        copy.wait()
    block_count, tiles = cols_ref.shape
    for tile in range(tiles):
        for b in range(block_count):
            table_ref[COLS + tile * block_count + b] = cols_ref[b, tile]
    slots = tile_ref.shape[0]
    for slot in range(slots):
        table_ref[NEEDS + slot] = tile_ref[slot]
        table_ref[NEEDS + slots + slot] = block_ref[slot]
    table_ref[NEEDS + 2 * slots] = count_ref[0]
    table_ref[PLACE] = place_ref[0]
    for k in range(len(OFFSETS)):
        for h in range(HALO):
            table_ref[k * HALO + h] = rows_ref[h, k]
    for copy in copies[:2]:
        copy.wait()
    for tile in range(tiles):
        target = jnp.concatenate(
            [target_ref[tile, pl.ds(v, NOBJ, stride=NVAR), :] for v in range(NVAR)], axis=0
        )
        sorted_ref[tile] = target
        state = relaxed(None, target, mixing_ref, tile)
        state_ref[tile] = state
        payload_ref[tile] = state.astype(jnp.bfloat16)
    row = lax.broadcasted_iota(jnp.int32, payload_ref.shape[1:], 0)
    told = jnp.zeros(payload_ref.shape[1:], jnp.float32)
    for k in range(len(OFFSETS)):
        for h in range(HALO):
            told = jnp.where(row == k * HALO + h, rows_ref[h, k].astype(jnp.float32), told)
    payload_ref[tiles] = told.astype(jnp.bfloat16)


def update_tiles(
    table_ref, state_ref, extended_ref, target_ref, mixing_ref, blocks_ref, store, before=None
):
    block_count = blocks_ref.shape[1]
    cells = blocks_ref.shape[3]
    for tile in range(state_ref.shape[0]):
        if before is not None:
            before(tile)
        first = COLS + tile * block_count
        picked = jnp.concatenate(
            [extended_ref[table_ref[first + b]] for b in range(block_count)], axis=1
        )
        product = jnp.dot(
            picked,
            blocks_ref[tile].reshape(block_count * cells, cells),
            preferred_element_type=jnp.float32,
        )
        current = state_ref[tile]
        residual = target_ref[tile] - (current + product)
        store(tile, relaxed(current, residual, mixing_ref, tile))


def pack(place, needs, rounded_ref, own_ref, layer_ref):
    rows = rounded_ref.shape[1]

    def wanted(offset, h):
        index = jnp.int32(0)
        for k, o in enumerate(OFFSETS):
            index = jnp.where(offset == o, needs[k * HALO + h], index)
        return index

    for h in range(HALO):
        span = slice(h * rows, (h + 1) * rows)
        for peer in range(LINE):
            own_ref[peer, span, :] = rounded_ref[wanted(peer - place, h)]
        for side in range(2):
            there = jnp.where(place < 2, side - 2, side + LINE)
            layer_ref[side, span, :] = rounded_ref[wanted(there - place, h)]


def second_kernel(
    mixing_hbm,
    blocks_hbm,
    rows_ref,
    state_ref,
    rounded_ref,
    from0_ref,
    from1_ref,
    from2_ref,
    from3_ref,
    target_ref,
    new_ref,
    new_rounded_ref,
    own_ref,
    layer_ref,
    table_ref,
    mixing_ref,
    blocks_ref,
    extended_ref,
    told_ref,
    sems,
):
    tiles = state_ref.shape[0]
    number = iter(range(sems.shape[0]))
    sources = (from0_ref, from1_ref, from2_ref, from3_ref)
    copies = []
    for k, source_ref in enumerate(sources):
        copies.append(
            pltpu.make_async_copy(source_ref.at[tiles], told_ref.at[k], sems.at[next(number)])
        )
        for h in range(HALO):
            entry = k * HALO + h
            copies.append(
                pltpu.make_async_copy(
                    source_ref.at[rows_ref[entry]],
                    extended_ref.at[tiles + entry],
                    sems.at[next(number)],
                )
            )
    large = pltpu.make_async_copy(mixing_hbm, mixing_ref, sems.at[next(number)])
    parts = []
    for start in range(0, tiles, PART):
        span = pl.ds(start, PART)
        parts.append(
            pltpu.make_async_copy(
                blocks_hbm.at[span], blocks_ref.at[span], sems.at[next(number)]
            )
        )
    for copy in parts + [large] + copies:
        copy.start()
    for tile in range(tiles):
        extended_ref[tile] = rounded_ref[tile]
    for entry in range(NEEDS, table_ref.shape[0]):
        table_ref[entry] = rows_ref[entry]
    for copy in copies:
        copy.wait()
    needs = [None] * NEEDS
    for k in range(len(sources)):
        named = told_ref[k].astype(jnp.float32)
        row = lax.broadcasted_iota(jnp.int32, named.shape, 0)
        told = OFFSETS.index(-OFFSETS[k])
        for h in range(HALO):
            entry = told * HALO + h
            needs[entry] = jnp.max(jnp.where(row == entry, named, 0.0)).astype(jnp.int32)
    for entry, need in enumerate(needs):
        table_ref[entry] = need
    large.wait()

    def before(tile):
        if tile % PART == 0:
            parts[tile // PART].wait()

    def store(tile, state):
        new_ref[tile] = state
        new_rounded_ref[tile] = state.astype(jnp.bfloat16)

    update_tiles(
        rows_ref, state_ref, extended_ref, target_ref, mixing_ref, blocks_ref, store, before
    )
    pack(rows_ref[PLACE], needs, new_rounded_ref, own_ref, layer_ref)


def design_sum(table_ref, state_ref, derivative_ref, weights_ref, sum_ref):
    owners = sum_ref.shape[0] // FB_DEV
    rows = NOBJ * NDIR
    slots = weights_ref.shape[0]
    sum_ref[...] = jnp.zeros(sum_ref.shape, jnp.float32)
    for slot in range(slots):
        selected = state_ref[table_ref[NEEDS + slot]]
        pieces = []
        for k in range(NDIR):
            total = None
            for v in range(NVAR):
                term = (
                    selected[v * NOBJ : (v + 1) * NOBJ, :]
                    * derivative_ref[v * NDIR + k, slot : slot + 1, :]
                )
                total = term if total is None else total + term
            pieces.append(total)
        alive = slot < table_ref[NEEDS + 2 * slots]
        sensitivity = jnp.where(alive, jnp.concatenate(pieces, axis=0), 0.0)
        coarse = sensitivity.astype(jnp.bfloat16).astype(jnp.float32)
        halves = lax.dot_general(
            jnp.concatenate([coarse, sensitivity - coarse], axis=0).astype(jnp.bfloat16),
            weights_ref[slot],
            (((1,), (1,)), ((), ())),
            preferred_element_type=jnp.float32,
        )
        block = table_ref[NEEDS + slots + slot]
        chunk = (block % FB_DEV) * owners + block // FB_DEV
        sum_ref[chunk] = sum_ref[chunk] + (halves[:rows] + halves[rows:])


def design_kernel(
    table_ref,
    state_ref,
    derivative_hbm,
    weights_hbm,
    partial_ref,
    derivative_ref,
    weights_ref,
    sum_ref,
    sems,
):
    pairs = ((derivative_hbm, derivative_ref), (weights_hbm, weights_ref))
    copies = [pltpu.make_async_copy(*pair, sems.at[i]) for i, pair in enumerate(pairs)]
    for copy in copies:
        copy.start()
    for copy in copies:
        copy.wait()
    design_sum(table_ref, state_ref, derivative_ref, weights_ref, sum_ref)
    partial_ref[...] = sum_ref[...].astype(jnp.bfloat16)


def sweep_kernel(kind, *refs):
    table_ref, state_ref, rounded_ref, halo_ref, target_ref, mixing_ref, blocks_ref = refs[:7]
    refs = list(refs[7:])
    copies = []
    if kind != "middle":
        derivative_hbm, weights_hbm = refs[:2]
        refs = refs[2:]
        sems = refs.pop()
        sum_ref, weights_ref, derivative_ref = refs.pop(), refs.pop(), refs.pop()
        copies.append(pltpu.make_async_copy(derivative_hbm, derivative_ref, sems.at[0]))
        copies.append(pltpu.make_async_copy(weights_hbm, weights_ref, sems.at[1]))
    extended_ref = refs.pop()
    if kind == "last":
        earlier_hbm, adjoint_hbm, chunks_ref = refs[:3]
        new_ref, adjoint_ref = refs[3:]
        half = sum_ref.shape[0]
        copies.append(
            pltpu.make_async_copy(earlier_hbm, chunks_ref.at[pl.ds(0, half)], sems.at[2])
        )
    else:
        new_ref, new_rounded_ref, own_ref, layer_ref = refs
    for copy in copies:
        copy.start()
    tiles = state_ref.shape[0]
    rows = state_ref.shape[1]
    place = table_ref[PLACE]
    for k, offset in enumerate(OFFSETS):
        source = place - offset
        relayed = jnp.where((source < 0) | (source >= LINE), 1, 0)
        peer = source & (LINE - 1)
        for h in range(HALO):
            start = pl.multiple_of((relayed * HALO + h) * rows, 16)
            extended_ref[tiles + k * HALO + h] = halo_ref[peer, pl.ds(start, rows), :]
    for tile in range(tiles):
        extended_ref[tile] = rounded_ref[tile]

    def store(tile, state):
        new_ref[tile] = state
        if kind == "last":
            for v in range(NVAR):
                part = state[v * NOBJ : (v + 1) * NOBJ, :]
                adjoint_ref[tile, pl.ds(v, NOBJ, stride=NVAR), :] = part
        else:
            new_rounded_ref[tile] = state.astype(jnp.bfloat16)

    update_tiles(table_ref, state_ref, extended_ref, target_ref, mixing_ref, blocks_ref, store)
    if kind == "last":
        written = pltpu.make_async_copy(adjoint_ref, adjoint_hbm, sems.at[3])
        written.start()
    if kind != "middle":
        for copy in copies:
            copy.wait()
        design_sum(table_ref, new_ref, derivative_ref, weights_ref, sum_ref)
    if kind == "last":
        chunks_ref[pl.ds(half, half)] = sum_ref[...].astype(jnp.bfloat16)
    else:
        needs = [table_ref[entry] for entry in range(NEEDS)]
        pack(place, needs, new_rounded_ref, own_ref, layer_ref)
    if kind != "middle":
        written.wait()


def in_hbm(value):
    return pltpu.with_memory_space_constraint(value, HBM)


def in_smem(value):
    return pltpu.with_memory_space_constraint(value, SMEM)


def first_sweep(place, rows, cols, indices, target, mixing):
    shape = jax.ShapeDtypeStruct(target.shape, jnp.float32)
    payload = jax.ShapeDtypeStruct((target.shape[0] + 1,) + target.shape[1:], jnp.bfloat16)
    table = SMEM((COLS + cols.size,), jnp.int32)
    small = (rows, cols) + indices[:2]
    large = (target, mixing)
    return pl.pallas_call(
        first_kernel,
        out_shape=(shape, shape, payload, table),
        in_specs=specs(*[HBM] * 6, SMEM, SMEM),
        out_specs=tuple(specs(VMEM, VMEM, VMEM, SMEM)),
        scratch_shapes=[pltpu.SMEM(value.shape, value.dtype) for value in small]
        + [pltpu.VMEM(value.shape, value.dtype) for value in large]
        + [pltpu.SemaphoreType.DMA((6,))],
        compiler_params=GRANT,
        name="first_sweep",
    )(*[in_hbm(value) for value in small + large], indices[2], place)


def sweep_shapes(state):
    chunk = (HALO * state.shape[1], state.shape[2])
    return (
        jax.ShapeDtypeStruct(state.shape, jnp.float32),
        jax.ShapeDtypeStruct(state.shape, jnp.bfloat16),
        jax.ShapeDtypeStruct((LINE,) + chunk, jnp.bfloat16),
        jax.ShapeDtypeStruct((2,) + chunk, jnp.bfloat16),
    )


def extended_scratch(state):
    return pltpu.VMEM((state.shape[0] + NEEDS,) + state.shape[1:], jnp.bfloat16)


def second_sweep(table, state, payload, sources, target, mixing, blocks):
    kept = (mixing, blocks)
    tiles = state.shape[0]
    copies = 1 + tiles // PART + NEEDS + len(OFFSETS)
    return pl.pallas_call(
        second_kernel,
        out_shape=sweep_shapes(state) + (SMEM(table.shape, table.dtype),),
        in_specs=specs(HBM, HBM, SMEM, VMEM, VMEM, *[pl.ANY] * 4, VMEM),
        out_specs=tuple(specs(VMEM, VMEM, VMEM, VMEM, SMEM)),
        scratch_shapes=[pltpu.VMEM(value.shape, value.dtype) for value in kept]
        + [
            extended_scratch(state),
            pltpu.VMEM((len(OFFSETS),) + state.shape[1:], jnp.bfloat16),
            pltpu.SemaphoreType.DMA((copies,)),
        ],
        compiler_params=GRANT,
        name="second_sweep",
    )(*[in_hbm(value) for value in kept], in_smem(table), state, payload, *sources, target)


def sweep(kind, table, state, rounded, halo, target, mixing, blocks, design=()):
    shapes = sweep_shapes(state)
    scratch = [extended_scratch(state)]
    in_specs = specs(SMEM, VMEM, VMEM, VMEM, VMEM, VMEM, VMEM)
    out_specs = specs(VMEM, VMEM, VMEM, VMEM)
    if kind != "middle":
        derivative, weights = design[:2]
        design = [in_hbm(value) for value in design]
        sums = (FB_DEV * lax.axis_size("sub"), NOBJ * NDIR, weights.shape[1])
        extra = [
            pltpu.VMEM(derivative.shape, derivative.dtype),
            pltpu.VMEM(weights.shape, weights.dtype),
            pltpu.VMEM(sums, jnp.float32),
            pltpu.SemaphoreType.DMA((4,)),
        ]
        in_specs += specs(HBM, HBM)
    if kind == "last":
        in_specs += specs(HBM)
        chunks = jax.ShapeDtypeStruct((OUTER * sums[0],) + sums[1:], jnp.bfloat16)
        shapes = (shapes[0], chunks)
        out_specs = specs(HBM, VMEM)
        full = pltpu.VMEM(state.shape, jnp.float32)
        scratch = [full, full] + scratch + extra
    return pl.pallas_call(
        functools.partial(sweep_kernel, kind),
        out_shape=shapes,
        in_specs=in_specs,
        out_specs=tuple(out_specs),
        scratch_shapes=scratch,
        compiler_params=GRANT,
        name="sweep_" + kind,
    )(in_smem(table), state, rounded, halo, target, mixing, blocks, *design)


def design_partial(table, state, derivative, weights):
    sums = (FB_DEV * lax.axis_size("sub"), NOBJ * NDIR, weights.shape[1])
    return pl.pallas_call(
        design_kernel,
        out_shape=HBM(sums, jnp.bfloat16),
        in_specs=specs(SMEM, VMEM, HBM, HBM),
        out_specs=pl.BlockSpec(memory_space=VMEM),
        scratch_shapes=[
            pltpu.VMEM(derivative.shape, derivative.dtype),
            pltpu.VMEM(weights.shape, weights.dtype),
            pltpu.VMEM(sums, jnp.float32),
            pltpu.SemaphoreType.DMA((2,)),
        ],
        compiler_params=GRANT,
        name="design_partial",
    )(in_smem(table), state, in_hbm(derivative), in_hbm(weights))


def exchange(own, layer, beside=None):
    count = lax.axis_size("dom")
    steps = [LINE if source % LINE >= 2 else -LINE for source in range(count)]
    pairs = [(source, (source + step) % count) for source, step in enumerate(steps)]
    relayed = lax.ppermute(layer, "dom", pairs)
    if beside is not None:
        relayed, beside = lax.optimization_barrier((relayed, beside))
    chunks = jnp.concatenate([own, jnp.concatenate([relayed, relayed], axis=0)], axis=1)
    lines = [[start + x for x in range(LINE)] for start in range(0, count, LINE)]
    return lax.all_to_all(chunks, "dom", 0, 0, axis_index_groups=lines), beside


def reduce_design(chunks, scaling):
    dom, sub = lax.axis_size("dom"), lax.axis_size("sub")
    part = OUTER * FB_DEV
    slabs = dom // part
    wide = part * sub
    groups = [[slab * wide + i for i in range(wide)] for slab in range(slabs)]
    spread = lax.all_to_all(chunks, ("dom", "sub"), 0, 0, axis_index_groups=groups)
    mine = jnp.sum(spread.astype(jnp.float32), axis=0)
    groups = [[slab * part + i for slab in range(slabs)] for i in range(part)]
    copies = jnp.broadcast_to(mine[None], (slabs,) + mine.shape)
    stacked = lax.all_to_all(copies, "dom", 0, 0, axis_index_groups=groups)
    total = jnp.sum(stacked, axis=0) * scaling
    groups = [[slab * part + i for i in range(part)] for slab in range(slabs)]
    copies = jnp.broadcast_to(total[None], (part,) + total.shape)
    gathered = lax.all_to_all(copies, "dom", 0, 0, axis_index_groups=groups)
    split = gathered.reshape(OUTER, FB_DEV, NDIR, NOBJ, gathered.shape[-1])
    return split.swapaxes(2, 3).reshape(OUTER, FB_DEV, NOBJ * NDIR, gathered.shape[-1])


def per_device(
    jac_blocks,
    block_cols,
    precond,
    right_side,
    halo_rows,
    surface_tile,
    surface_block,
    surface_count,
    surface_residual_derivative,
    lattice_bernstein_weights,
):
    slot_count = surface_tile.shape[0]
    scaling = math.sqrt(FB_DEV / (slot_count * lax.axis_size("dom")))
    cols = block_cols.T
    rows = halo_rows.T
    place = (lax.axis_index("dom") % LINE).astype(jnp.int32).reshape(1)
    indices = (surface_tile, surface_block, surface_count)
    design = (surface_residual_derivative.transpose(1, 0, 2), lattice_bernstein_weights)
    target, state, payload, table = first_sweep(
        place, rows, cols, indices, right_side, precond
    )
    sources = [from_behind(payload, "dom", offset) for offset in OFFSETS]
    state, rounded, own, layer, table = second_sweep(
        table, state, payload, sources, target, precond, jac_blocks
    )
    count = OUTER * INNER
    for number in range(2, count):
        beside = partial if number == INNER else None
        halo, beside = exchange(own, layer, beside)
        if beside is not None:
            partial = beside
        arrays = (table, state, rounded, halo, target, precond, jac_blocks)
        if number == count - 1:
            adjoint, chunks = sweep("last", *arrays, design + (partial,))
        else:
            state, rounded, own, layer = sweep("middle", *arrays)
        if number == INNER - 1:
            partial = design_partial(table, state, *design)
    return (adjoint, reduce_design(chunks, scaling))


def solution(mesh):
    in_specs = (
        P(("dom", "sub"), None, None, None),
        P(("dom", "sub"), None),
        P(("dom", "sub"), None, None),
        P(("dom", "sub"), None, None),
        P(("dom", "sub"), None),
        P(("dom", "sub")),
        P(("dom", "sub")),
        P(("dom", "sub")),
        P(("dom", "sub"), None, None),
        P(("dom", "sub"), None, None),
    )
    out_specs = (P(("dom", "sub"), None, None), P(None, "sub", None, None))
    return jax.shard_map(
        per_device, mesh=mesh, in_specs=in_specs, out_specs=out_specs, check_vma=False
    )
```

```python
import functools
import math

import jax
import jax.numpy as jnp
from jax import lax
from jax.experimental import pallas as pl
from jax.experimental.pallas import tpu as pltpu
from jax.sharding import PartitionSpec as P

NOBJ = 8
NVAR = 6
NDIR = 3
FB_DEV = 4
OUTER = 2
INNER = 5
HALO = 2
LINE = 4

OFFSETS = (1, -1, 2, -2)
NEEDS = len(OFFSETS) * HALO
COLS = 32
PLACE = COLS - 1
PART = 3
RELAXATION = 0.7
VMEM = pltpu.MemorySpace.VMEM
SMEM = pltpu.MemorySpace.SMEM
HBM = pltpu.MemorySpace.HBM
GRANT = pltpu.CompilerParams(vmem_limit_bytes=16 * 1024 * 1024)


def specs(*kinds):
    return [pl.BlockSpec(memory_space=kind) for kind in kinds]


def from_behind(value, axis, steps):
    count = lax.axis_size(axis)
    pairs = [(source, (source + steps) % count) for source in range(count)]
    return lax.ppermute(value, axis, pairs)


def relaxed(current, residual, mixing_ref, tile):
    rows = [residual[w * NOBJ : (w + 1) * NOBJ, :] for w in range(NVAR)]
    pieces = []
    for v in range(NVAR):
        total = RELAXATION * rows[v]
        for w in range(NVAR):
            k = v * NVAR + w
            total = total + mixing_ref[tile, k : k + 1, :] * rows[w]
        pieces.append(total)
    update = jnp.concatenate(pieces, axis=0)
    return update if current is None else current + update


def first_kernel(
    rows_hbm,
    cols_hbm,
    tile_hbm,
    block_hbm,
    target_hbm,
    mixing_hbm,
    count_ref,
    place_ref,
    sorted_ref,
    state_ref,
    payload_ref,
    table_ref,
    rows_ref,
    cols_ref,
    tile_ref,
    block_ref,
    target_ref,
    mixing_ref,
    sems,
):
    pairs = (
        (target_hbm, target_ref),
        (mixing_hbm, mixing_ref),
        (rows_hbm, rows_ref),
        (cols_hbm, cols_ref),
        (tile_hbm, tile_ref),
        (block_hbm, block_ref),
    )
    copies = [pltpu.make_async_copy(*pair, sems.at[i]) for i, pair in enumerate(pairs)]
    for copy in copies:
        copy.start()
    for copy in copies[2:]:
        copy.wait()
    block_count, tiles = cols_ref.shape
    for tile in range(tiles):
        for b in range(block_count):
            table_ref[COLS + tile * block_count + b] = cols_ref[b, tile]
    slots = tile_ref.shape[0]
    for slot in range(slots):
        table_ref[NEEDS + slot] = tile_ref[slot]
        table_ref[NEEDS + slots + slot] = block_ref[slot]
    table_ref[NEEDS + 2 * slots] = count_ref[0]
    table_ref[PLACE] = place_ref[0]
    for k in range(len(OFFSETS)):
        for h in range(HALO):
            table_ref[k * HALO + h] = rows_ref[h, k]
    for copy in copies[:2]:
        copy.wait()
    for tile in range(tiles):
        target = jnp.concatenate(
            [target_ref[tile, pl.ds(v, NOBJ, stride=NVAR), :] for v in range(NVAR)], axis=0
        )
        sorted_ref[tile] = target
        state = relaxed(None, target, mixing_ref, tile)
        state_ref[tile] = state
        payload_ref[tile] = state.astype(jnp.bfloat16)
    row = lax.broadcasted_iota(jnp.int32, payload_ref.shape[1:], 0)
    told = jnp.zeros(payload_ref.shape[1:], jnp.float32)
    for k in range(len(OFFSETS)):
        for h in range(HALO):
            told = jnp.where(row == k * HALO + h, rows_ref[h, k].astype(jnp.float32), told)
    payload_ref[tiles] = told.astype(jnp.bfloat16)


def update_tiles(
    table_ref, state_ref, extended_ref, target_ref, mixing_ref, blocks_ref, store, before=None
):
    block_count = blocks_ref.shape[1]
    cells = blocks_ref.shape[3]
    for tile in range(state_ref.shape[0]):
        if before is not None:
            before(tile)
        first = COLS + tile * block_count
        picked = jnp.concatenate(
            [extended_ref[table_ref[first + b]] for b in range(block_count)], axis=1
        )
        product = jnp.dot(
            picked,
            blocks_ref[tile].reshape(block_count * cells, cells),
            preferred_element_type=jnp.float32,
        )
        current = state_ref[tile]
        residual = target_ref[tile] - (current + product)
        store(tile, relaxed(current, residual, mixing_ref, tile))


def pack(place, needs, rounded_ref, own_ref, layer_ref):
    rows = rounded_ref.shape[1]

    def wanted(offset, h):
        index = jnp.int32(0)
        for k, o in enumerate(OFFSETS):
            index = jnp.where(offset == o, needs[k * HALO + h], index)
        return index

    for h in range(HALO):
        span = slice(h * rows, (h + 1) * rows)
        for peer in range(LINE):
            own_ref[peer, span, :] = rounded_ref[wanted(peer - place, h)]
        for side in range(2):
            there = jnp.where(place < 2, side - 2, side + LINE)
            layer_ref[side, span, :] = rounded_ref[wanted(there - place, h)]


def second_kernel(
    mixing_hbm,
    blocks_hbm,
    rows_ref,
    state_ref,
    rounded_ref,
    from0_ref,
    from1_ref,
    from2_ref,
    from3_ref,
    target_ref,
    new_ref,
    new_rounded_ref,
    own_ref,
    layer_ref,
    table_ref,
    mixing_ref,
    blocks_ref,
    extended_ref,
    told_ref,
    sems,
):
    tiles = state_ref.shape[0]
    number = iter(range(sems.shape[0]))
    sources = (from0_ref, from1_ref, from2_ref, from3_ref)
    copies = []
    for k, source_ref in enumerate(sources):
        copies.append(
            pltpu.make_async_copy(
                source_ref.at[tiles, pl.ds(0, 16)], told_ref.at[k], sems.at[next(number)]
            )
        )
        for h in range(HALO):
            entry = k * HALO + h
            copies.append(
                pltpu.make_async_copy(
                    source_ref.at[rows_ref[entry]],
                    extended_ref.at[tiles + entry],
                    sems.at[next(number)],
                )
            )
    large = pltpu.make_async_copy(mixing_hbm, mixing_ref, sems.at[next(number)])
    parts = []
    for start in range(0, tiles, PART):
        span = pl.ds(start, PART)
        parts.append(
            pltpu.make_async_copy(
                blocks_hbm.at[span], blocks_ref.at[span], sems.at[next(number)]
            )
        )
    for copy in copies + [large] + parts:
        copy.start()
    for tile in range(tiles):
        extended_ref[tile] = rounded_ref[tile]
    for entry in range(NEEDS, table_ref.shape[0]):
        table_ref[entry] = rows_ref[entry]
    for copy in copies:
        copy.wait()
    needs = [None] * NEEDS
    for k in range(len(sources)):
        named = told_ref[k].astype(jnp.float32)[:NEEDS]
        row = lax.broadcasted_iota(jnp.int32, named.shape, 0)
        told = OFFSETS.index(-OFFSETS[k])
        for h in range(HALO):
            entry = told * HALO + h
            needs[entry] = jnp.max(jnp.where(row == entry, named, 0.0)).astype(jnp.int32)
    for entry, need in enumerate(needs):
        table_ref[entry] = need
    large.wait()

    def before(tile):
        if tile % PART == 0:
            parts[tile // PART].wait()

    def store(tile, state):
        new_ref[tile] = state
        new_rounded_ref[tile] = state.astype(jnp.bfloat16)

    update_tiles(
        rows_ref, state_ref, extended_ref, target_ref, mixing_ref, blocks_ref, store, before
    )
    pack(rows_ref[PLACE], needs, new_rounded_ref, own_ref, layer_ref)


def design_sum(table_ref, state_ref, derivative_ref, weights_ref, sum_ref):
    owners = sum_ref.shape[0] // FB_DEV
    rows = NOBJ * NDIR
    slots = weights_ref.shape[0]
    sum_ref[...] = jnp.zeros(sum_ref.shape, jnp.float32)
    for slot in range(slots):
        selected = state_ref[table_ref[NEEDS + slot]]
        pieces = []
        for k in range(NDIR):
            total = None
            for v in range(NVAR):
                term = (
                    selected[v * NOBJ : (v + 1) * NOBJ, :]
                    * derivative_ref[v * NDIR + k, slot : slot + 1, :]
                )
                total = term if total is None else total + term
            pieces.append(total)
        alive = slot < table_ref[NEEDS + 2 * slots]
        sensitivity = jnp.where(alive, jnp.concatenate(pieces, axis=0), 0.0)
        coarse = sensitivity.astype(jnp.bfloat16).astype(jnp.float32)
        halves = lax.dot_general(
            jnp.concatenate([coarse, sensitivity - coarse], axis=0).astype(jnp.bfloat16),
            weights_ref[slot],
            (((1,), (1,)), ((), ())),
            preferred_element_type=jnp.float32,
        )
        block = table_ref[NEEDS + slots + slot]
        chunk = (block % FB_DEV) * owners + block // FB_DEV
        sum_ref[chunk] = sum_ref[chunk] + (halves[:rows] + halves[rows:])


def design_kernel(
    table_ref,
    state_ref,
    derivative_hbm,
    weights_hbm,
    partial_ref,
    derivative_ref,
    weights_ref,
    sum_ref,
    sems,
):
    pairs = ((derivative_hbm, derivative_ref), (weights_hbm, weights_ref))
    copies = [pltpu.make_async_copy(*pair, sems.at[i]) for i, pair in enumerate(pairs)]
    for copy in copies:
        copy.start()
    for copy in copies:
        copy.wait()
    design_sum(table_ref, state_ref, derivative_ref, weights_ref, sum_ref)
    partial_ref[...] = sum_ref[...].astype(jnp.bfloat16)


def sweep_kernel(kind, *refs):
    table_ref, state_ref, rounded_ref, halo_ref, target_ref, mixing_ref, blocks_ref = refs[:7]
    refs = list(refs[7:])
    copies = []
    if kind != "middle":
        derivative_hbm, weights_hbm = refs[:2]
        refs = refs[2:]
        sems = refs.pop()
        sum_ref, weights_ref, derivative_ref = refs.pop(), refs.pop(), refs.pop()
        copies.append(pltpu.make_async_copy(derivative_hbm, derivative_ref, sems.at[0]))
        copies.append(pltpu.make_async_copy(weights_hbm, weights_ref, sems.at[1]))
    extended_ref = refs.pop()
    if kind == "last":
        earlier_hbm, adjoint_hbm, chunks_ref = refs[:3]
        new_ref, adjoint_ref = refs[3:]
        half = sum_ref.shape[0]
        copies.append(
            pltpu.make_async_copy(earlier_hbm, chunks_ref.at[pl.ds(0, half)], sems.at[2])
        )
    else:
        new_ref, new_rounded_ref, own_ref, layer_ref = refs
    for copy in copies:
        copy.start()
    tiles = state_ref.shape[0]
    rows = state_ref.shape[1]
    place = table_ref[PLACE]
    for k, offset in enumerate(OFFSETS):
        source = place - offset
        relayed = jnp.where((source < 0) | (source >= LINE), 1, 0)
        peer = source & (LINE - 1)
        for h in range(HALO):
            start = pl.multiple_of((relayed * HALO + h) * rows, 16)
            extended_ref[tiles + k * HALO + h] = halo_ref[peer, pl.ds(start, rows), :]
    for tile in range(tiles):
        extended_ref[tile] = rounded_ref[tile]

    def store(tile, state):
        new_ref[tile] = state
        if kind == "last":
            for v in range(NVAR):
                part = state[v * NOBJ : (v + 1) * NOBJ, :]
                adjoint_ref[tile, pl.ds(v, NOBJ, stride=NVAR), :] = part
        else:
            new_rounded_ref[tile] = state.astype(jnp.bfloat16)

    update_tiles(table_ref, state_ref, extended_ref, target_ref, mixing_ref, blocks_ref, store)
    if kind == "last":
        written = pltpu.make_async_copy(adjoint_ref, adjoint_hbm, sems.at[3])
        written.start()
    if kind != "middle":
        for copy in copies:
            copy.wait()
        design_sum(table_ref, new_ref, derivative_ref, weights_ref, sum_ref)
    if kind == "last":
        chunks_ref[pl.ds(half, half)] = sum_ref[...].astype(jnp.bfloat16)
    else:
        needs = [table_ref[entry] for entry in range(NEEDS)]
        pack(place, needs, new_rounded_ref, own_ref, layer_ref)
    if kind != "middle":
        written.wait()


def in_hbm(value):
    return pltpu.with_memory_space_constraint(value, HBM)


def in_smem(value):
    return pltpu.with_memory_space_constraint(value, SMEM)


def first_sweep(place, rows, cols, indices, target, mixing):
    shape = jax.ShapeDtypeStruct(target.shape, jnp.float32)
    payload = jax.ShapeDtypeStruct((target.shape[0] + 1,) + target.shape[1:], jnp.bfloat16)
    table = SMEM((COLS + cols.size,), jnp.int32)
    small = (rows, cols) + indices[:2]
    large = (target, mixing)
    return pl.pallas_call(
        first_kernel,
        out_shape=(shape, shape, payload, table),
        in_specs=specs(*[HBM] * 6, SMEM, SMEM),
        out_specs=tuple(specs(VMEM, VMEM, VMEM, SMEM)),
        scratch_shapes=[pltpu.SMEM(value.shape, value.dtype) for value in small]
        + [pltpu.VMEM(value.shape, value.dtype) for value in large]
        + [pltpu.SemaphoreType.DMA((6,))],
        compiler_params=GRANT,
        name="first_sweep",
    )(*[in_hbm(value) for value in small + large], indices[2], place)


def sweep_shapes(state):
    chunk = (HALO * state.shape[1], state.shape[2])
    return (
        jax.ShapeDtypeStruct(state.shape, jnp.float32),
        jax.ShapeDtypeStruct(state.shape, jnp.bfloat16),
        jax.ShapeDtypeStruct((LINE,) + chunk, jnp.bfloat16),
        jax.ShapeDtypeStruct((2,) + chunk, jnp.bfloat16),
    )


def extended_scratch(state):
    return pltpu.VMEM((state.shape[0] + NEEDS,) + state.shape[1:], jnp.bfloat16)


def second_sweep(table, state, payload, sources, target, mixing, blocks):
    kept = (mixing, blocks)
    tiles = state.shape[0]
    copies = 1 + tiles // PART + NEEDS + len(OFFSETS)
    return pl.pallas_call(
        second_kernel,
        out_shape=sweep_shapes(state) + (SMEM(table.shape, table.dtype),),
        in_specs=specs(HBM, HBM, SMEM, VMEM, VMEM, *[pl.ANY] * 4, VMEM),
        out_specs=tuple(specs(VMEM, VMEM, VMEM, VMEM, SMEM)),
        scratch_shapes=[pltpu.VMEM(value.shape, value.dtype) for value in kept]
        + [
            extended_scratch(state),
            pltpu.VMEM((len(OFFSETS), 16, state.shape[2]), jnp.bfloat16),
            pltpu.SemaphoreType.DMA((copies,)),
        ],
        compiler_params=GRANT,
        name="second_sweep",
    )(*[in_hbm(value) for value in kept], in_smem(table), state, payload, *sources, target)


def sweep(kind, table, state, rounded, halo, target, mixing, blocks, design=()):
    shapes = sweep_shapes(state)
    scratch = [extended_scratch(state)]
    in_specs = specs(SMEM, VMEM, VMEM, VMEM, VMEM, VMEM, VMEM)
    out_specs = specs(VMEM, VMEM, VMEM, VMEM)
    if kind != "middle":
        derivative, weights = design[:2]
        design = [in_hbm(value) for value in design]
        sums = (FB_DEV * lax.axis_size("sub"), NOBJ * NDIR, weights.shape[1])
        extra = [
            pltpu.VMEM(derivative.shape, derivative.dtype),
            pltpu.VMEM(weights.shape, weights.dtype),
            pltpu.VMEM(sums, jnp.float32),
            pltpu.SemaphoreType.DMA((4,)),
        ]
        in_specs += specs(HBM, HBM)
    if kind == "last":
        in_specs += specs(HBM)
        chunks = jax.ShapeDtypeStruct((OUTER * sums[0],) + sums[1:], jnp.bfloat16)
        shapes = (shapes[0], chunks)
        out_specs = specs(HBM, VMEM)
        full = pltpu.VMEM(state.shape, jnp.float32)
        scratch = [full, full] + scratch + extra
    return pl.pallas_call(
        functools.partial(sweep_kernel, kind),
        out_shape=shapes,
        in_specs=in_specs,
        out_specs=tuple(out_specs),
        scratch_shapes=scratch,
        compiler_params=GRANT,
        name="sweep_" + kind,
    )(in_smem(table), state, rounded, halo, target, mixing, blocks, *design)


def design_partial(table, state, derivative, weights):
    sums = (FB_DEV * lax.axis_size("sub"), NOBJ * NDIR, weights.shape[1])
    return pl.pallas_call(
        design_kernel,
        out_shape=HBM(sums, jnp.bfloat16),
        in_specs=specs(SMEM, VMEM, HBM, HBM),
        out_specs=pl.BlockSpec(memory_space=VMEM),
        scratch_shapes=[
            pltpu.VMEM(derivative.shape, derivative.dtype),
            pltpu.VMEM(weights.shape, weights.dtype),
            pltpu.VMEM(sums, jnp.float32),
            pltpu.SemaphoreType.DMA((2,)),
        ],
        compiler_params=GRANT,
        name="design_partial",
    )(in_smem(table), state, in_hbm(derivative), in_hbm(weights))


def exchange(own, layer, beside=None):
    count = lax.axis_size("dom")
    steps = [LINE if source % LINE >= 2 else -LINE for source in range(count)]
    pairs = [(source, (source + step) % count) for source, step in enumerate(steps)]
    relayed = lax.ppermute(layer, "dom", pairs)
    if beside is not None:
        relayed, beside = lax.optimization_barrier((relayed, beside))
    chunks = jnp.concatenate([own, jnp.concatenate([relayed, relayed], axis=0)], axis=1)
    lines = [[start + x for x in range(LINE)] for start in range(0, count, LINE)]
    return lax.all_to_all(chunks, "dom", 0, 0, axis_index_groups=lines), beside


def reduce_design(chunks, scaling):
    dom, sub = lax.axis_size("dom"), lax.axis_size("sub")
    part = OUTER * FB_DEV
    slabs = dom // part
    wide = part * sub
    groups = [[slab * wide + i for i in range(wide)] for slab in range(slabs)]
    spread = lax.all_to_all(chunks, ("dom", "sub"), 0, 0, axis_index_groups=groups)
    mine = jnp.sum(spread.astype(jnp.float32), axis=0)
    groups = [[slab * part + i for slab in range(slabs)] for i in range(part)]
    copies = jnp.broadcast_to(mine[None], (slabs,) + mine.shape)
    stacked = lax.all_to_all(copies, "dom", 0, 0, axis_index_groups=groups)
    total = jnp.sum(stacked, axis=0) * scaling
    groups = [[slab * part + i for i in range(part)] for slab in range(slabs)]
    copies = jnp.broadcast_to(total[None], (part,) + total.shape)
    gathered = lax.all_to_all(copies, "dom", 0, 0, axis_index_groups=groups)
    split = gathered.reshape(OUTER, FB_DEV, NDIR, NOBJ, gathered.shape[-1])
    return split.swapaxes(2, 3).reshape(OUTER, FB_DEV, NOBJ * NDIR, gathered.shape[-1])


def per_device(
    jac_blocks,
    block_cols,
    precond,
    right_side,
    halo_rows,
    surface_tile,
    surface_block,
    surface_count,
    surface_residual_derivative,
    lattice_bernstein_weights,
):
    slot_count = surface_tile.shape[0]
    scaling = math.sqrt(FB_DEV / (slot_count * lax.axis_size("dom")))
    cols = block_cols.T
    rows = halo_rows.T
    place = (lax.axis_index("dom") % LINE).astype(jnp.int32).reshape(1)
    indices = (surface_tile, surface_block, surface_count)
    design = (surface_residual_derivative.transpose(1, 0, 2), lattice_bernstein_weights)
    target, state, payload, table = first_sweep(
        place, rows, cols, indices, right_side, precond
    )
    sources = [from_behind(payload, "dom", offset) for offset in OFFSETS]
    state, rounded, own, layer, table = second_sweep(
        table, state, payload, sources, target, precond, jac_blocks
    )
    count = OUTER * INNER
    for number in range(2, count):
        beside = partial if number == INNER else None
        halo, beside = exchange(own, layer, beside)
        if beside is not None:
            partial = beside
        arrays = (table, state, rounded, halo, target, precond, jac_blocks)
        if number == count - 1:
            adjoint, chunks = sweep("last", *arrays, design + (partial,))
        else:
            state, rounded, own, layer = sweep("middle", *arrays)
        if number == INNER - 1:
            partial = design_partial(table, state, *design)
    return (adjoint, reduce_design(chunks, scaling))


def solution(mesh):
    in_specs = (
        P(("dom", "sub"), None, None, None),
        P(("dom", "sub"), None),
        P(("dom", "sub"), None, None),
        P(("dom", "sub"), None, None),
        P(("dom", "sub"), None),
        P(("dom", "sub")),
        P(("dom", "sub")),
        P(("dom", "sub")),
        P(("dom", "sub"), None, None),
        P(("dom", "sub"), None, None),
    )
    out_specs = (P(("dom", "sub"), None, None), P(None, "sub", None, None))
    return jax.shard_map(
        per_device, mesh=mesh, in_specs=in_specs, out_specs=out_specs, check_vma=False
    )
```
